128 devices in a mesh: row: 8 (over x, core), col: 16 (over z, y).
Axes of the slice: x: 4, y: 4, z: 4, core: 2. Of those that a mesh axis runs over, the one named last changes fastest.
Arguments:
- amplitudes: bfloat16 [16, 16, 512, 512], P(None, 'row', 'col'), may hold values from -6 to 6
- integrals: bfloat16 [16, 512, 16, 512], P('row', 'col'), may hold values from -0.09375 to 0.09375
- occupancy: int32 [16, 16, 4, 4], replicated, may hold values from 0 to 1, as said below
Outputs:
- cycle: bfloat16 [16, 16, 512, 512], P('col', 'row')
The draws below stay inside these ranges and needn't reach their ends.
Inputs may be any that keep to these rules, and one draw needn't show every extreme that they name: occupancy[i, k, s, t] is 1 where tile s of the first virtual index and tile t of the second are kept for the pair (i, k), else 0; it is always 1 for i = k.
All inputs are finite; a program needn't handle non-finite values.
Results may differ from the reference program's by a relative error of at most 0.001.
Values may be sent and summed in bfloat16 or wider, within the bound.
No kernel may reach another device: no remote copies, remote signals or barrier semaphores. Data moves between devices by JAX's collectives and lax.ppermute only.
A program may use at most 128 MiB of HBM per device.

```python
import jax
import jax.numpy as jnp
from jax import lax

NO = 16
DOM = 4
TILE = 128
DT = 512


def draw_occupancy(key, part):
    levels = jax.random.randint(key, (NO, NO, DOM, DOM), 0, NO)
    first_index = jnp.arange(NO, dtype=jnp.int32)[:, None, None, None]
    second_index = jnp.arange(NO, dtype=jnp.int32)[None, :, None, None]
    distance = jnp.abs(first_index - second_index)
    return (levels >= distance).astype(jnp.int32)


def strengthened(result, key, source, target, parts, factor):
    def block_of(position):
        return (jnp.arange(result.shape[position]) // (result.shape[position] // parts)).reshape((-1,) + (1,) * (result.ndim - 1 - position))

    one_side = jax.random.permutation(key, parts)[block_of(target)]
    other_side = (block_of(target) + parts // 2) % parts
    return jnp.where((block_of(source) == one_side) | (block_of(source) == other_side), factor * result, result)


def block_levels(rng, extent, cuts, smallest, largest):
    def one(dim, blocks):
        heights = jax.random.uniform(jax.random.fold_in(jax.random.fold_in(rng, 6), dim), (blocks,), jnp.float32, smallest / len(cuts), largest / len(cuts))
        return jnp.repeat(jnp.exp(heights), extent[dim] // blocks).reshape((-1,) + (1,) * (len(extent) - dim - 1))

    level = one(*cuts[0])
    for cut in cuts[1:]:
        level = level * one(*cut)
    return level


def bell_draw(rng, extent, scale, limit, split=(), kind=jnp.bfloat16):
    level = block_levels(rng, extent, split, -0.22, 0.18) if split else 1.0
    drawn = jax.random.normal(rng, extent, jnp.float32) * scale * level
    return jnp.minimum(jnp.maximum(drawn, -limit), limit).astype(kind)


def heavy_noise(rng, extent, spread, most, cuts, heavy, kind=jnp.bfloat16):
    drawn = spread * jax.random.normal(rng, extent, jnp.float32)
    if cuts:
        drawn = drawn * block_levels(rng, extent, cuts, -0.22, 0.18)
    return jnp.clip(strengthened(drawn, jax.random.fold_in(rng, 3), *heavy), -most, most).astype(kind)


def setup_inputs(seed: int = 0) -> dict:
    streams_of = jax.random.split(jax.random.key(seed), 4)
    return {
        "amplitudes": bell_draw(streams_of[0], (NO, NO, DT, DT), 1.0, 6.0, ((1, 8), (2, 16))),
        "integrals": heavy_noise(streams_of[1], (NO, DT, NO, DT), (NO * DOM * TILE) ** -0.5, 0.09375, ((0, 8), (1, 16)), (1, 2, 16, 2.0)),
        "occupancy": draw_occupancy(jax.random.fold_in(streams_of[3], 71), 0),
    }


def reference(amplitudes, integrals, occupancy):
    expanded = jnp.repeat(jnp.repeat(occupancy, TILE, axis=2), TILE, axis=3)
    screened = amplitudes * expanded.astype(jnp.bfloat16)
    size_total = NO * DOM * TILE
    left_matrix = jnp.transpose(screened.astype(jnp.float32), (0, 3, 1, 2)).reshape(size_total, size_total)
    right_matrix = integrals.astype(jnp.float32).reshape(size_total, size_total)
    product = jnp.dot(left_matrix, right_matrix, precision=lax.Precision.HIGHEST, preferred_element_type=jnp.float32)
    product = product.reshape(NO, DOM * TILE, NO, DOM * TILE)
    return jnp.transpose(product, (2, 0, 3, 1)).astype(jnp.bfloat16)
```

```python
import jax
import jax.numpy as jnp
from jax import lax
from jax.experimental import pallas as pl
from jax.experimental.pallas import tpu as pltpu
from jax.sharding import PartitionSpec as P

TILE = 128
SHIFTS = (0, 1, 3, 2)


def x_move(value, shift):
    pairs = [(2 * x + h, 2 * ((x + shift) % 4) + h) for x in range(4) for h in range(2)]
    return lax.ppermute(value, "row", pairs)


def core_swap(value):
    return lax.ppermute(value, "row", [(r, r ^ 1) for r in range(8)])


def y_move(value, shift):
    pairs = [(4 * z + y, 4 * z + (y + shift) % 4) for z in range(4) for y in range(4)]
    return lax.ppermute(value, "col", pairs)


def z_move(value, shift):
    pairs = [(4 * z + y, 4 * ((z + shift) % 4) + y) for z in range(4) for y in range(4)]
    return lax.ppermute(value, "col", pairs)


def screen_body(place, occupancy, amp_ref, out_ref):
    d, e = pl.program_id(0), pl.program_id(1)
    x, h, z = place[0], place[1], place[2]
    shift = jnp.where(d == 2, 3, jnp.where(d == 3, 2, d))
    first = 4 * ((x + shift) % 4) + 2 * jnp.where(e == 0, h, 1 - h)
    for i in range(2):
        for k in range(2):
            for t in range(4):
                kept = occupancy[first + i, (2 * x + h) * 2 + k, z, t].astype(jnp.float32)
                part = amp_ref[i, k, :, TILE * t : TILE * (t + 1)].astype(jnp.float32)
                out_ref[0, 0, i, k, :, TILE * t : TILE * (t + 1)] = (part * kept).astype(jnp.bfloat16)


def screen(place, occupancy, amplitudes):
    def amp_block(d, e, place, occupancy):
        shift = jnp.where(d == 2, 3, jnp.where(d == 3, 2, d))
        return (2 * ((place[0] + shift) % 4) + jnp.where(e == 0, place[1], 1 - place[1]), 0, 0, 0)

    return pl.pallas_call(
        screen_body,
        out_shape=jax.ShapeDtypeStruct((4, 2, 2, 2, 32, 512), jnp.bfloat16),
        grid_spec=pltpu.PrefetchScalarGridSpec(
            num_scalar_prefetch=2,
            grid=(4, 2),
            in_specs=[pl.BlockSpec((2, 2, 32, 512), amp_block)],
            out_specs=pl.BlockSpec((1, 1, 2, 2, 32, 512), lambda d, e, *_: (d, e, 0, 0, 0, 0)),
        ),
        cost_estimate=pl.CostEstimate(flops=1 << 19, bytes_accessed=1 << 21, transcendentals=0),
    )(place, occupancy, amplitudes)


def ring(value, move, axis):
    forth, back = move(value, 1), move(value, -1)
    far = (move(forth[:1], 1), move(back[1:], -1))
    return value, forth, back, far


def joined(pieces, axis):
    value, forth, back, far = pieces
    return jnp.stack([value, forth, back, jnp.concatenate(far, axis=0)], axis=axis)


def per_device(amplitudes, integrals, occupancy):
    row, col = lax.axis_index("row"), lax.axis_index("col")
    x, h, z, y = row // 2, row % 2, col // 4, col % 4
    place = jnp.stack([x, h, z, y]).astype(jnp.int32)

    by_orbital = jnp.transpose(integrals, (2, 0, 1, 3)).reshape(4, 4, 2, 32, 512)
    over_z = []
    for shift in SHIFTS:
        piece = lax.dynamic_index_in_dim(by_orbital, (z + shift) % 4, 0, keepdims=False)
        over_z.append(z_move(piece, shift) if shift else piece)
    over_y = []
    for shift in SHIFTS:
        piece = jnp.stack([lax.dynamic_index_in_dim(p, (y + shift) % 4, 0, keepdims=False) for p in over_z])
        over_y.append(y_move(piece, shift) if shift else piece)
    held = jnp.stack(over_y)
    forth, back = x_move(held, 1), x_move(held, -1)
    far = jnp.concatenate([x_move(forth[:2], 1), x_move(back[2:], -1)], axis=0)
    mine = [held, forth, back, far]
    other = [core_swap(p) for p in mine]
    b_mine = jnp.stack(mine).transpose(2, 0, 1, 3, 4, 5).reshape(4, 1024, 512)
    b_other = jnp.stack(other, axis=0).transpose(1, 0, 2, 3, 4, 5).reshape(4, 1024, 512)
    b_mine = jnp.stack(mine).transpose(2, 0, 1, 3, 4, 5).reshape(4, 1024, 512)

    ready = screen(place, occupancy, amplitudes)
    arrived = [x_move(ready[d], shift) if shift else ready[d] for d, shift in enumerate(SHIFTS)]
    half_own = jnp.stack([p[0] for p in arrived], axis=1)
    half_other = core_swap(jnp.stack([p[1] for p in arrived], axis=1))

    own = joined(ring(half_own, y_move, 0), 2)
    oth = joined(ring(half_other, z_move, 0), 2)
    total = [None, None]

    def add(i, left, right):
        product = lax.dot_general(
            right, left.reshape(1024, 512), (((0,), (0,)), ((), ())), preferred_element_type=jnp.float32
        )
        total[i] = product if total[i] is None else total[i] + product

    chunks = [(ring(own, z_move, 0), b_mine), (ring(oth, y_move, 0), b_other)]
    for step in range(3):
        for pieces, right in chunks:
            for i in range(2):
                add(i, pieces[step][i], right[step])
    for pieces, right in chunks:
        for i in range(2):
            add(i, pieces[3][i][0], right[3])
    return jnp.stack(total)[None].astype(jnp.bfloat16)


def solution(mesh):
    in_specs = (P(None, "row", "col", None), P("row", "col", None, None), P())
    out_specs = P("col", "row", None, None)
    return jax.shard_map(
        per_device, mesh=mesh, in_specs=in_specs, out_specs=out_specs, check_vma=False
    )
```

```python
import jax
import jax.numpy as jnp
from jax import lax
from jax.experimental import pallas as pl
from jax.experimental.pallas import tpu as pltpu
from jax.sharding import PartitionSpec as P


TILE = 128
SHIFTS = (0, 1, 3, 2)


def x_move(value, shift):
    pairs = [(2 * x + h, 2 * ((x + shift) % 4) + h) for x in range(4) for h in range(2)]
    return lax.ppermute(value, "row", pairs)


def core_swap(value):
    return lax.ppermute(value, "row", [(r, r ^ 1) for r in range(8)])


def y_move(value, shift):
    pairs = [(4 * z + y, 4 * z + (y + shift) % 4) for z in range(4) for y in range(4)]
    return lax.ppermute(value, "col", pairs)


def z_move(value, shift):
    pairs = [(4 * z + y, 4 * ((z + shift) % 4) + y) for z in range(4) for y in range(4)]
    return lax.ppermute(value, "col", pairs)


def screen_body(occ_ref, amp_ref, *out_refs):
    row, col = lax.axis_index("row"), lax.axis_index("col")
    x, h, z = row // 2, row % 2, col // 4
    table = occ_ref[:, pl.ds(z, 1), :, :].reshape(16, 4, 16)
    orbital = lax.broadcasted_iota(jnp.int32, (16, 4, 16), 2)
    for k in range(2):
        kept = jnp.sum(jnp.where(orbital == 2 * row + k, table, 0), axis=2, keepdims=True)
        mask_ref = out_refs[4]
        mask_ref[k] = jnp.broadcast_to(kept.astype(jnp.float32), (16, 4, TILE))
    for d, shift in enumerate(SHIFTS):
        for e in range(2):
            first = 4 * ((x + shift) % 4) + 2 * (h if e == 0 else 1 - h)
            for i in range(2):
                for k in range(2):
                    rows = out_refs[4][k, first + i]
                    for t in range(4):
                        part = amp_ref[first + i, k, :, TILE * t : TILE * (t + 1)]
                        keep = jnp.broadcast_to(rows[t : t + 1], (32, TILE)).astype(jnp.bfloat16)
                        out_refs[d][e, i, k, :, TILE * t : TILE * (t + 1)] = part * keep


def screen(occupancy, amplitudes):
    piece = jax.ShapeDtypeStruct((2, 2, 2, 32, 512), jnp.bfloat16)
    vmem = pl.BlockSpec(memory_space=pltpu.VMEM)
    return pl.pallas_call(
        screen_body,
        out_shape=[piece] * 4,
        in_specs=[vmem, vmem],
        out_specs=[vmem] * 4,
        scratch_shapes=[pltpu.VMEM((2, 16, 4, TILE), jnp.float32)],
        cost_estimate=pl.CostEstimate(flops=1 << 19, bytes_accessed=1 << 21, transcendentals=0),
    )(jnp.transpose(occupancy, (0, 2, 3, 1)), amplitudes)


def ring(value, move):
    forth = move(value, 1)
    back = move(value, -1)
    far_forth = move(forth[:, 0], 1)
    far_back = move(back[:, 1], -1)
    return [[value[:, i], forth[:, i], back[:, i], (far_forth, far_back)[i]] for i in range(2)]


def split_ring(values, move):
    near = [[None, None], [None, None]]
    for way, order in (("forth", (0, 1)), ("back", (1, 0))):
        for i in order:
            near[i][0 if way == "forth" else 1] = move(values[i], 1 if way == "forth" else -1)
    far = [move(near[0][0], 1), move(near[1][1], -1)]
    return [[values[i], near[i][0], near[i][1], far[i]] for i in range(2)]


def per_device(amplitudes, integrals, occupancy):
    col = lax.axis_index("col")
    z, y = col // 4, col % 4

    ready = screen(occupancy, amplitudes)
    arrived = [x_move(ready[d], shift) if shift else ready[d] for d, shift in enumerate(SHIFTS)]

    by_orbital = jnp.transpose(integrals, (2, 0, 1, 3)).reshape(4, 4, 2, 32, 512)
    over_z = []
    for shift in SHIFTS:
        piece = lax.dynamic_index_in_dim(by_orbital, (z + shift) % 4, 0, keepdims=False)
        over_z.append(z_move(piece, shift) if shift else piece)
    over_y = []
    for shift in SHIFTS:
        piece = jnp.stack([lax.dynamic_index_in_dim(p, (y + shift) % 4, 0, keepdims=False) for p in over_z])
        over_y.append(y_move(piece, shift) if shift else piece)
    held = jnp.stack(over_y)
    forth, back = x_move(held, 1), x_move(held, -1)
    far = jnp.concatenate([x_move(forth[:2], 1), x_move(back[2:], -1)], axis=0)
    mine = [held, forth, back, far]
    other = []
    for piece in mine:
        other.append(core_swap(piece))
    b_mine = jnp.stack(mine).transpose(2, 1, 0, 3, 4, 5).reshape(4, 1024, 512)
    b_other = jnp.stack(other).transpose(1, 2, 0, 3, 4, 5).reshape(4, 1024, 512)

    half_own = jnp.stack([p[0] for p in arrived])
    half_other = core_swap(jnp.stack([p[1] for p in arrived]))
    own = [jnp.stack(p) for p in ring(half_own, y_move)]
    oth = [jnp.stack(p) for p in ring(half_other, z_move)]
    own_pieces = split_ring(own, z_move)
    oth_pieces = split_ring(oth, y_move)

    outs = []
    for i in range(2):
        total = None
        for step in (0, 1 + i, 2 - i, 3):
            for pieces, right in ((own_pieces, b_mine), (oth_pieces, b_other)):
                left = pieces[i][step].reshape(1024, 512)
                product = lax.dot_general(
                    right[step], left, (((0,), (0,)), ((), ())), preferred_element_type=jnp.float32
                )
                total = product if total is None else total + product
        outs.append(total.astype(jnp.bfloat16))
    return jnp.stack(outs)[None]


def solution(mesh):
    in_specs = (P(None, "row", "col", None), P("row", "col", None, None), P())
    out_specs = P("col", "row", None, None)
    return jax.shard_map(per_device, mesh=mesh, in_specs=in_specs, out_specs=out_specs, check_vma=False)
```
